512 devices in a mesh: loop: 32 (over z, y_hi), seg: 16 (over x, y_lo, core).
Axes of the slice: x: 4, y: 4 (y_hi: 2, y_lo: 2; y = y_hi * 2 + y_lo), z: 16, core: 2. Of those that a mesh axis runs over, the one named last changes fastest.
Arguments:
- dosage: bfloat16 [8192, 32768], P('seg', 'loop'), may hold values from -3 to 3
- weight_tiles: bfloat16 [3, 1024, 4096], P(None, None, 'loop'), may hold values from -0.109375 to 0.109375
- first_tile: int32 [4096], P('loop'), may hold values from 0 to 1
- last_tile: int32 [4096], P('loop'), may hold values from 1 to 2
Outputs:
- covariance: float32 [4096, 4096], P('seg', 'loop')
The draws below stay inside these ranges and needn't reach their ends.
Inputs may be any that keep to these rules, and one draw needn't show every extreme that they name: `first_tile`: a gene's window always covers its home slot 1.
All inputs are finite; a program needn't handle non-finite values.
Results may differ from the reference program's by a relative error of at most 0.0021.
Values may be sent and summed in bfloat16 or wider, within the bound.
A program may use at most 64 MiB of HBM per device.

```python
import jax
import jax.numpy as jnp
from jax import lax

BLOCK = 1024
GENE_DEV = 128
REACH = 1
SPAN = 3
SAMPLES = 8192
VARIANTS = 32768
GENES = 4096


def touch_ends(array, own_key, smallest, top_value):
    shape = array.shape
    index_at = [jax.random.randint(jax.random.fold_in(own_key, axis), (), 0, shape[axis]) for axis in range(len(shape))]
    array = array.at[tuple(index_at)].set(smallest)
    longest = shape.index(max(shape))
    index_at[longest] = (index_at[longest] + 1) % shape[longest]
    return array.at[tuple(index_at)].set(top_value)


def block_scale(own_key, shape, cuts, least, largest):
    def one(axis_at, shards_of):
        steps = jax.random.uniform(jax.random.fold_in(jax.random.fold_in(own_key, 6), axis_at), (shards_of,), jnp.float32, least / len(cuts), largest / len(cuts))
        return jnp.repeat(jnp.exp(steps), shape[axis_at] // shards_of).reshape((-1,) + (1,) * (len(shape) - axis_at - 1))

    gain = one(*cuts[0])
    for cut in cuts[1:]:
        gain = gain * one(*cut)
    return gain


def gaussian(own_key, shape, width, most, cuts=(), held_as=jnp.bfloat16):
    gain = block_scale(own_key, shape, cuts, -0.22, 0.18) if cuts else 1.0
    values = jax.random.normal(own_key, shape, jnp.float32) * width * gain
    return jnp.minimum(jnp.maximum(values, -most), most).astype(held_as)


def setup_inputs(seed: int = 0) -> dict:
    streams_of = jax.random.split(jax.random.key(seed), 5)
    return {
        "dosage": gaussian(streams_of[0], (SAMPLES, VARIANTS), 0.6, 3.0, ((0, 16), (1, 32))),
        "weight_tiles": gaussian(streams_of[1], (SPAN, BLOCK, GENES), (SPAN * BLOCK) ** -0.5, 0.109375, ((2, 32),)),
        "first_tile": touch_ends(jax.random.randint(streams_of[2], (GENES,), 0, REACH + 1), jax.random.fold_in(streams_of[2], 1), 0, REACH).astype(jnp.int32),
        "last_tile": touch_ends(jax.random.randint(streams_of[3], (GENES,), REACH, SPAN), jax.random.fold_in(streams_of[3], 1), REACH, SPAN - 1).astype(jnp.int32),
    }


def reference(dosage, weight_tiles, first_tile, last_tile):
    blocks = VARIANTS // BLOCK
    slot_index = jnp.arange(SPAN, dtype=jnp.int32)[:, None]
    covered = (slot_index >= first_tile[None, :]) & (slot_index <= last_tile[None, :])
    masked = jnp.where(covered[:, None, :], weight_tiles, jnp.zeros((), weight_tiles.dtype))

    def one_block(home_block):
        running = jnp.zeros((SAMPLES, GENE_DEV), jnp.float32)
        for slot_pos in range(SPAN):
            source = home_block + slot_pos - REACH
            inside = (source >= 0) & (source < blocks)
            col_first = (jnp.clip(source, 0, blocks - 1) * BLOCK).astype(jnp.int32)
            columns = lax.dynamic_slice(dosage, (jnp.int32(0), col_first), (SAMPLES, BLOCK))
            gene_first = (home_block * GENE_DEV).astype(jnp.int32)
            moved_tile = lax.dynamic_slice(masked[slot_pos], (jnp.int32(0), gene_first), (BLOCK, GENE_DEV))
            pair_term = jnp.dot(columns, moved_tile, preferred_element_type=jnp.float32)
            running = running + jnp.where(inside, pair_term, jnp.zeros((), jnp.float32))
        return running.astype(jnp.bfloat16)

    pieces = lax.map(one_block, jnp.arange(blocks, dtype=jnp.int32))
    projection = jnp.transpose(pieces, (1, 0, 2)).reshape(SAMPLES, GENES)
    summed = lax.dot_general(projection, projection, (((0,), (0,)), ((), ())), preferred_element_type=jnp.float32)
    return summed / SAMPLES
```

```python
import functools

import jax
import jax.numpy as jnp
from jax import lax
from jax.experimental import pallas as pl
from jax.experimental.pallas import tpu as pltpu
from jax.sharding import PartitionSpec as P

MESH = pl.DeviceIdType.MESH
F32 = jnp.float32
BF16 = jnp.bfloat16
XS, ZS = 4, 16


def device(x, t, lo, z, c):
    return {"loop": 2 * z + t, "seg": 4 * x + 2 * lo + c}


def kernel(
    dosage, tiles, first, last, out,
    mine, send_a, send_b, tile_a, tile_b,
    part_y, part_z, got_y, got_z, held,
    columns, rows, shares, across, summed, arrived, landed,
    wsend, wrecv, csend, crecv, psend, precv,
    qsend, qrecv, rsend, rrecv, osend, orecv,
    xsend, xrecv, ysend, yrecv,
):
    loop, seg = lax.axis_index("loop"), lax.axis_index("seg")
    z, t = loop // 2, loop % 2
    x, lo, c = seg // 4, (seg // 2) % 2, seg % 2
    sign = 1 - 2 * t
    z_fore, z_back = (z + sign + ZS) % ZS, (z - sign + ZS) % ZS
    fore, back = device(x, t, lo, z_fore, c), device(x, t, lo, z_back, c)
    twin = device(x, t, lo, z, 1 - c)
    pair = device(x, 1 - t, lo, z, c)
    near = device(x, 1 - t, 1 - lo, z, c)
    near_back = device(x, 1 - t, 1 - lo, z_back, c)
    side = device(x, t, 1 - lo, z, c)
    half = dosage.shape[0] // 2
    depth = dosage.shape[1]
    gene = tiles.shape[2]

    barrier = pltpu.get_barrier_semaphore()
    partners = [fore, back, twin, pair, near, near_back, side]
    partners += [device((x + k) % XS, t, lo, z, c) for k in range(1, XS)]
    for partner in partners:
        pl.semaphore_signal(barrier, inc=1, device_id=partner, device_id_type=MESH)

    def remote(src, dst, send, recv, to):
        return pltpu.make_async_remote_copy(
            src_ref=src, dst_ref=dst, send_sem=send, recv_sem=recv,
            device_id=to, device_id_type=MESH,
        )

    low, high = first[...], last[...]

    def mask(slot):
        block = loop + slot - 1
        ok = (low <= slot) & (high >= slot) & (block >= 0) & (block < 2 * ZS)
        return jnp.where(ok, 1.0, 0.0).astype(BF16)

    piece = pl.ds(pl.multiple_of(c * (depth // 2), depth // 2), depth // 2)
    slot_b, slot_a = 2 * t, 2 - 2 * t
    send_b[...] = tiles[slot_b, piece, :] * mask(slot_b)
    send_a[...] = tiles[slot_a, piece, :] * mask(slot_a)
    pl.semaphore_wait(barrier, len(partners))

    weights = []
    for i, (src, dst, to) in enumerate(
        ((send_b, tile_b, near_back), (send_a, tile_a, near))
    ):
        copy = remote(src, dst.at[piece], wsend.at[i], wrecv.at[i], to)
        copy.start()
        weights.append(copy)
    mine[...] = tiles[1] * mask(1)
    partials = []
    for k in range(2):
        span = pl.ds(k * half, half)
        part_y[span, :] = jnp.dot(dosage[span, :], mine[...], preferred_element_type=F32)
        copy = remote(part_y.at[span], got_y.at[span], psend.at[k], precv.at[k], pair)
        copy.start()
        partials.append(copy)

    swaps = []
    for i, dst in enumerate((tile_b, tile_a)):
        weights[i].wait_recv()
        copy = remote(dst.at[piece], dst.at[piece], csend.at[i], crecv.at[i], twin)
        copy.start()
        swaps.append(copy)
        copy.wait_recv()
        for k in range(2):
            span = pl.ds(k * half, half)
            value = jnp.dot(dosage[span, :], dst[...], preferred_element_type=F32)
            if i == 0:
                part_z[span, :] = value
                copy = remote(part_z.at[span], got_z.at[span], psend.at[2 + k], precv.at[2 + k], back)
                copy.start()
                partials.append(copy)
            else:
                held[span, :] = value

    lead = (z + c) % 2 == 0
    cols_own = pl.ds(pl.multiple_of((1 - t) * gene, gene), gene)
    cols_other = pl.ds(pl.multiple_of(t * gene, gene), gene)
    place = z // 2

    def ring(block, flow, step, j, to):
        chunk = rows.at[block, j]
        return remote(
            chunk, chunk, rsend.at[flow, step // 2, j], rrecv.at[flow, (step + 1) // 2, j], to
        )

    def start_ring(j):
        ring(place, 0, 0, j, fore).start()
        ring(place, 1, 0, j, back).start()

    locals_ = []
    for k in range(2):
        span = pl.ds(k * half, half)
        partials[k].wait_recv()
        partials[2 + k].wait_recv()
        value = held[span, :] + got_y[span, :] + got_z[span, :]
        columns[span, cols_own] = value.astype(BF16)
        turned = value.T.astype(BF16)

        @pl.when(lead)
        def _():
            rows[place, k] = turned
            start_ring(k)

        @pl.when(jnp.logical_not(lead))
        def _():
            landed[k] = turned
            remote(landed.at[k], rows.at[place, 2 + k], osend.at[k], orecv.at[k], twin).start()

        here = columns.at[span, cols_own]
        copy = remote(here, here, qsend.at[0, k], qrecv.at[0, k], pair)
        copy.start()
        locals_.append(copy)
        there = columns.at[pl.ds(2 * half + k * half, half), cols_own]
        copy = remote(here, there, qsend.at[1, k], qrecv.at[1, k], twin)
        copy.start()
        locals_.append(copy)

    @pl.when(lead)
    def _():
        for k in range(2):
            remote(landed.at[k], rows.at[place, 2 + k], osend.at[k], orecv.at[k], twin).wait_recv()
            start_ring(2 + k)

    relays = []
    for k in range(2):
        span = pl.ds(k * half, half)
        got = columns.at[span, cols_other]
        remote(got, got, qsend.at[0, k], qrecv.at[0, k], pair).wait_recv()
        there = columns.at[pl.ds(2 * half + k * half, half), cols_other]
        copy = remote(got, there, qsend.at[2, k], qrecv.at[2, k], twin)
        copy.start()
        relays.append(copy)
    for copy in (locals_[1], locals_[3], *relays):
        copy.wait_recv()

    def share(block):
        turned = jnp.concatenate([rows[block, j] for j in range(4)], axis=1)
        shares[block] = jnp.dot(turned, columns[...], preferred_element_type=F32)
        home = block // 2

        @pl.when(home != x)
        def _():
            remote(
                shares.at[block], across.at[block % 2, x], xsend.at[block],
                xrecv.at[block % 2, x], device(home, t, lo, z, c),
            ).start()

    @pl.when(lead)
    def _():
        share(place)

    odd = (z + c) % 2

    def travel(i, carry):
        step = 2 * i + odd
        far = (z - sign * step + 2 * ZS) % ZS // 2
        close = (z + sign * step + 2 * ZS) % ZS // 2
        for j in range(4):
            @pl.when((step >= 1) & (step <= 8))
            def _():
                ring(far, 0, step - 1, j, fore).wait_recv()

            @pl.when((step >= 1) & (step <= 7))
            def _():
                ring(far, 0, step, j, fore).start()
                ring(close, 1, step - 1, j, back).wait_recv()

            @pl.when((step >= 1) & (step <= 6))
            def _():
                ring(close, 1, step, j, back).start()

        @pl.when((step >= 1) & (step <= 8))
        def _():
            share(far)

        @pl.when((step >= 1) & (step <= 7))
        def _():
            share(close)

        return carry

    lax.fori_loop(0, 5, travel, 0)

    for other in range(2):
        block = 2 * x + other
        total = shares[block]
        for k in range(1, XS):
            source = (x + k) % XS
            remote(
                shares.at[block], across.at[other, source], xsend.at[block],
                xrecv.at[other, source], twin,
            ).wait_recv()
            total = total + across[other, source]
        for way in range(2):
            summed[other, way] = total[:, way * gene:(way + 1) * gene]
    outs = []
    for flip_t, flip_lo, index in ((1, 0, 0), (0, 1, 1), (1, 1, 2)):
        to_t, to_lo = (t + flip_t) % 2, (lo + flip_lo) % 2
        copy = remote(
            summed.at[to_lo, to_t], arrived.at[index], ysend.at[index], yrecv.at[index],
            device(x, to_t, to_lo, z, c),
        )
        copy.start()
        outs.append(copy)
    scale = 1.0 / (2 * half * XS * 4)
    own_rows = pl.ds(pl.multiple_of((1 - t) * gene, gene), gene)
    other_rows = pl.ds(pl.multiple_of(t * gene, gene), gene)
    outs[1].wait_recv()
    out[own_rows, :] = (summed[lo, t] + arrived[1]) * scale
    outs[0].wait_recv()
    outs[2].wait_recv()
    out[other_rows, :] = (arrived[0] + arrived[2]) * scale

    for copy in (*weights, *swaps, *partials, *locals_, *relays, *outs):
        copy.wait_send()

    @pl.when(jnp.logical_not(lead))
    def _():
        for k in range(2):
            remote(landed.at[k], rows.at[place, 2 + k], osend.at[k], orecv.at[k], twin).wait_send()

    @pl.when(lead)
    def _():
        for j in range(4):
            ring(place, 0, 0, j, fore).wait_send()
            ring(place, 1, 0, j, back).wait_send()

    def drain(i, carry):
        step = 2 * i + odd
        for j in range(4):
            @pl.when((step >= 1) & (step <= 7))
            def _():
                ring(place, 0, step, j, fore).wait_send()

            @pl.when((step >= 1) & (step <= 6))
            def _():
                ring(place, 1, step, j, back).wait_send()

        return carry

    lax.fori_loop(0, 4, drain, 0)

    def drain_shares(block, carry):
        @pl.when(block // 2 != x)
        def _():
            remote(
                shares.at[block], across.at[0, 0], xsend.at[block], xrecv.at[0, 0], twin
            ).wait_send()

        return carry

    lax.fori_loop(0, ZS // 2, drain_shares, 0)


def shards(dosage, weight_tiles, first_tile, last_tile):
    samples, depth = dosage.shape
    gene = weight_tiles.shape[2]
    half = samples // 2
    dma = pltpu.SemaphoreType.DMA
    vmem = pl.BlockSpec(memory_space=pltpu.VMEM)
    return pl.pallas_call(
        kernel,
        out_shape=jax.ShapeDtypeStruct((2 * gene, gene), F32),
        in_specs=[vmem] * 4,
        out_specs=vmem,
        scratch_shapes=[
            pltpu.VMEM((depth, gene), BF16),
            pltpu.VMEM((depth // 2, gene), BF16),
            pltpu.VMEM((depth // 2, gene), BF16),
            pltpu.VMEM((depth, gene), BF16),
            pltpu.VMEM((depth, gene), BF16),
            pltpu.VMEM((samples, gene), F32),
            pltpu.VMEM((samples, gene), F32),
            pltpu.VMEM((samples, gene), F32),
            pltpu.VMEM((samples, gene), F32),
            pltpu.VMEM((samples, gene), F32),
            pltpu.VMEM((2 * samples, 2 * gene), BF16),
            pltpu.VMEM((ZS // 2, 4, gene, half), BF16),
            pltpu.VMEM((ZS // 2, gene, 2 * gene), F32),
            pltpu.VMEM((2, XS, gene, 2 * gene), F32),
            pltpu.VMEM((2, 2, gene, gene), F32),
            pltpu.VMEM((3, gene, gene), F32),
            pltpu.VMEM((2, gene, half), BF16),
            dma((2,)), dma((2,)), dma((2,)), dma((2,)),
            dma((4,)), dma((4,)),
            dma((3, 2)), dma((3, 2)),
            dma((2, 5, 4)), dma((2, 5, 4)),
            dma((2,)), dma((2,)),
            dma((ZS // 2,)), dma((2, XS)),
            dma((3,)), dma((3,)),
        ],
        compiler_params=pltpu.CompilerParams(
            collective_id=0, has_side_effects=True, vmem_limit_bytes=40 * 2**20
        ),
    )(dosage, weight_tiles, first_tile.reshape(1, gene), last_tile.reshape(1, gene))


def solution(mesh):
    return jax.shard_map(
        shards,
        mesh=mesh,
        in_specs=(P("seg", "loop"), P(None, None, "loop"), P("loop"), P("loop")),
        out_specs=P("seg", "loop"),
        check_vma=False,
    )
```

```python
import functools

import jax
import jax.numpy as jnp
from jax import lax
from jax.experimental import pallas as pl
from jax.experimental.pallas import tpu as pltpu
from jax.sharding import PartitionSpec as P

MESH = pl.DeviceIdType.MESH
F32 = jnp.float32
BF16 = jnp.bfloat16
XS, ZS = 4, 16


def device(x, t, lo, z, c):
    return {"loop": 2 * z + t, "seg": 4 * x + 2 * lo + c}


ORDER = (0, 1, 4, 2, 5, 3, 6, 7)
PARTS = 4


def kernel(
    dosage_hbm, tiles_hbm, first_hbm, last_hbm, out,
    dosage, tiles, first, last,
    mine, send_a, send_b, tile_a, tile_b,
    part_y, part_z, got_y, got_z, held,
    columns, rows, shares, across, summed, arrived, landed,
    isem, wsend, wrecv, csend, crecv, psend, precv, zsend, zrecv,
    qsend, qrecv, rsend, rrecv, osend, orecv,
    xsend, xrecv, ysend, yrecv,
):
    loop, seg = lax.axis_index("loop"), lax.axis_index("seg")
    z, t = loop // 2, loop % 2
    x, lo, c = seg // 4, (seg // 2) % 2, seg % 2
    sign = 1 - 2 * t
    z_fore, z_back = (z + sign + ZS) % ZS, (z - sign + ZS) % ZS
    fore, back = device(x, t, lo, z_fore, c), device(x, t, lo, z_back, c)
    fore_twin, back_twin = device(x, t, lo, z_fore, 1 - c), device(x, t, lo, z_back, 1 - c)
    twin = device(x, t, lo, z, 1 - c)
    pair = device(x, 1 - t, lo, z, c)
    near = device(x, 1 - t, 1 - lo, z, c)
    near_back = device(x, 1 - t, 1 - lo, z_back, c)
    side = device(x, t, 1 - lo, z, c)
    samples, depth = dosage.shape
    gene = tiles.shape[2]
    part = samples // PARTS
    half = samples // 2

    barrier = pltpu.get_barrier_semaphore()
    partners = [fore, back, fore_twin, back_twin, twin, pair, near, near_back, side]
    partners += [device((x + k) % XS, t, lo, z, c) for k in range(1, XS)]
    for partner in partners:
        pl.semaphore_signal(barrier, inc=1, device_id=partner, device_id_type=MESH)

    piece = pl.ds(pl.multiple_of(c * (depth // 2), depth // 2), depth // 2)
    slot_b, slot_a = 2 * t, 2 - 2 * t
    loads = [
        pltpu.make_async_copy(src, dst, isem.at[i])
        for i, (src, dst) in enumerate((
            (first_hbm, first), (last_hbm, last),
            (tiles_hbm.at[slot_b, piece], tiles.at[slot_b, piece]),
            (tiles_hbm.at[slot_a, piece], tiles.at[slot_a, piece]),
            (tiles_hbm.at[1], tiles.at[1]), (dosage_hbm, dosage),
        ))
    ]
    for load in loads:
        load.start()

    def remote(src, dst, send, recv, to):
        return pltpu.make_async_remote_copy(
            src_ref=src, dst_ref=dst, send_sem=send, recv_sem=recv,
            device_id=to, device_id_type=MESH,
        )

    loads[0].wait()
    loads[1].wait()
    low, high = first[...], last[...]

    def mask(slot):
        block = loop + slot - 1
        ok = (low <= slot) & (high >= slot) & (block >= 0) & (block < 2 * ZS)
        return jnp.where(ok, 1.0, 0.0).astype(BF16)

    loads[2].wait()
    send_b[...] = tiles[slot_b, piece, :] * mask(slot_b)
    pl.semaphore_wait(barrier, len(partners))

    give_b = remote(send_b, tile_b.at[piece], wsend.at[0], wrecv.at[0], near_back)
    give_b.start()
    loads[3].wait()
    send_a[...] = tiles[slot_a, piece, :] * mask(slot_a)
    give_a = remote(send_a, tile_a.at[piece], wsend.at[1], wrecv.at[1], near)
    give_a.start()
    loads[4].wait()
    mine[...] = tiles[1] * mask(1)
    loads[5].wait()
    partials = []

    def send_partials():
        for k in range(2):
            span = pl.ds(k * half, half)
            copy = remote(part_y.at[span], got_y.at[span], psend.at[k], precv.at[k], pair)
            copy.start()
            partials.append(copy)

    part_y[...] = jnp.dot(dosage[...], mine[...], preferred_element_type=F32)
    swap_b = remote(tile_b.at[piece], tile_b.at[piece], csend.at[0], crecv.at[0], twin)
    swap_a = remote(tile_a.at[piece], tile_a.at[piece], csend.at[1], crecv.at[1], twin)
    give_b.wait_recv()
    swap_b.start()
    send_partials()
    swap_b.wait_recv()
    halos = []
    for k in range(PARTS):
        span = pl.ds(k * part, part)
        part_z[span, :] = jnp.dot(dosage[span, :], tile_b[...], preferred_element_type=F32)
        copy = remote(part_z.at[span], got_z.at[span], zsend.at[k], zrecv.at[k], back)
        copy.start()
        halos.append(copy)
    give_a.wait_recv()
    swap_a.start()
    swap_a.wait_recv()
    held[...] = jnp.dot(dosage[...], tile_a[...], preferred_element_type=F32)

    lead = (z + c) % 2 == 0
    cols_own = pl.ds(pl.multiple_of((1 - t) * gene, gene), gene)
    cols_other = pl.ds(pl.multiple_of(t * gene, gene), gene)
    place = z // 2

    def ring(block, flow, step, j, to):
        chunk = rows.at[block, j]
        return remote(
            chunk, chunk, rsend.at[flow, step // 2, j], rrecv.at[flow, (step + 1) // 2, j], to
        )

    def enter(k, flow, to):
        return remote(
            landed.at[k], rows.at[place, PARTS + k], osend.at[flow, k],
            rrecv.at[flow, 0, PARTS + k], to,
        )

    def enter_twin(k):
        return remote(
            landed.at[k], rows.at[place, PARTS + k], osend.at[2, k], orecv.at[k], twin
        )

    locals_ = []
    for k in range(PARTS):
        span = pl.ds(k * part, part)
        if k % 2 == 0:
            partials[k // 2].wait_recv()
        halos[k].wait_recv()
        value = held[span, :] + got_y[span, :] + got_z[span, :]
        turned = value.T.astype(BF16)

        @pl.when(lead)
        def _():
            rows[place, k] = turned
            ring(place, 0, 0, k, fore).start()
            ring(place, 1, 0, k, back).start()

        @pl.when(jnp.logical_not(lead))
        def _():
            landed[k] = turned
            enter(k, 0, fore_twin).start()
            enter(k, 1, back_twin).start()
            enter_twin(k).start()

        columns[span, cols_own] = value.astype(BF16)
        if k % 2 == 1:
            i = k // 2
            here = columns.at[pl.ds(i * half, half), cols_own]
            copy = remote(here, here, qsend.at[0, i], qrecv.at[0, i], pair)
            copy.start()
            locals_.append(copy)
            there = columns.at[pl.ds(samples + i * half, half), cols_own]
            copy = remote(here, there, qsend.at[1, i], qrecv.at[1, i], twin)
            copy.start()
            locals_.append(copy)

    def share(block):
        turned = jnp.concatenate([rows[block, j] for j in range(2 * PARTS)], axis=1)
        shares[block] = jnp.dot(turned, columns[...], preferred_element_type=F32)
        home = block // 2

        @pl.when(home != x)
        def _():
            remote(
                shares.at[block], across.at[block % 2, x], xsend.at[block],
                xrecv.at[block % 2, x], device(home, t, lo, z, c),
            ).start()

    odd = (z + c) % 2

    def pass_on(step, far, close):
        for j in ORDER:
            @pl.when((step >= 1) & (step <= 8))
            def _():
                ring(far, 0, step - 1, j, fore).wait_recv()

            @pl.when((step >= 1) & (step <= 7))
            def _():
                ring(far, 0, step, j, fore).start()
                ring(close, 1, step - 1, j, back).wait_recv()

            @pl.when((step >= 1) & (step <= 6))
            def _():
                ring(close, 1, step, j, back).start()

    def spots(step):
        return (z - sign * step + 2 * ZS) % ZS // 2, (z + sign * step + 2 * ZS) % ZS // 2

    pass_on(odd, *spots(odd))
    relays = []
    for i in range(2):
        got = columns.at[pl.ds(i * half, half), cols_other]
        remote(got, got, qsend.at[0, i], qrecv.at[0, i], pair).wait_recv()
        there = columns.at[pl.ds(samples + i * half, half), cols_other]
        copy = remote(got, there, qsend.at[2, i], qrecv.at[2, i], twin)
        copy.start()
        relays.append(copy)
    for copy in (locals_[1], locals_[3], *relays):
        copy.wait_recv()

    @pl.when(lead)
    def _():
        for k in range(PARTS):
            enter_twin(k).wait_recv()
        share(place)

    @pl.when(jnp.logical_not(lead))
    def _():
        for block in spots(1):
            share(block)

    def travel(i, carry):
        step = 2 * i + odd
        far, close = spots(step)
        pass_on(step, far, close)

        @pl.when(step <= 8)
        def _():
            share(far)

        @pl.when(step <= 7)
        def _():
            share(close)

        return carry

    lax.fori_loop(1, 5, travel, 0)

    def away(block):
        gap = (2 * block + c - z + ZS) % ZS
        return jnp.minimum(gap, ZS - gap)

    swapped = (away(2 * x) > away(2 * x + 1)).astype(jnp.int32)

    def ysend_copy(index, block_lo, to_t, to_lo):
        return remote(
            summed.at[block_lo, to_t], arrived.at[index], ysend.at[index], yrecv.at[index],
            device(x, to_t, to_lo, z, c),
        )

    same = ysend_copy(0, lo, 1 - t, lo)
    cross = ysend_copy(1, 1 - lo, t, 1 - lo)
    both = ysend_copy(2, 1 - lo, 1 - t, 1 - lo)
    for turn in range(2):
        other = (swapped + turn) % 2
        block = 2 * x + other
        for k in range(1, XS):
            source = (x + k) % XS
            remote(
                shares.at[block], across.at[other, source], xsend.at[block],
                xrecv.at[other, source], twin,
            ).wait_recv()
        total = shares[block]
        for k in range(1, XS):
            total = total + across[other, (x + k) % XS]
        for way in range(2):
            summed[other, way] = total[:, way * gene:(way + 1) * gene]

        @pl.when(other == lo)
        def _():
            same.start()

        @pl.when(other != lo)
        def _():
            both.start()
            cross.start()

    scale = 1.0 / (samples * XS * 4)
    own_rows = pl.ds(pl.multiple_of((1 - t) * gene, gene), gene)
    other_rows = pl.ds(pl.multiple_of(t * gene, gene), gene)
    cross.wait_recv()
    out[own_rows, :] = (summed[lo, t] + arrived[1]) * scale
    same.wait_recv()
    both.wait_recv()
    out[other_rows, :] = (arrived[0] + arrived[2]) * scale

    for copy in (
        give_a, give_b, swap_a, swap_b, *partials, *halos, *locals_, *relays, same, cross, both
    ):
        copy.wait_send()

    @pl.when(jnp.logical_not(lead))
    def _():
        for k in range(PARTS):
            enter(k, 0, fore_twin).wait_send()
            enter(k, 1, back_twin).wait_send()
            enter_twin(k).wait_send()

    @pl.when(lead)
    def _():
        for k in range(PARTS):
            ring(place, 0, 0, k, fore).wait_send()
            ring(place, 1, 0, k, back).wait_send()

    def drain(i, carry):
        step = 2 * i + odd
        for j in range(2 * PARTS):
            @pl.when((step >= 1) & (step <= 7))
            def _():
                ring(place, 0, step, j, fore).wait_send()

            @pl.when((step >= 1) & (step <= 6))
            def _():
                ring(place, 1, step, j, back).wait_send()

        return carry

    lax.fori_loop(0, 4, drain, 0)

    def drain_shares(block, carry):
        @pl.when(block // 2 != x)
        def _():
            remote(
                shares.at[block], across.at[0, 0], xsend.at[block], xrecv.at[0, 0], twin
            ).wait_send()

        return carry

    lax.fori_loop(0, ZS // 2, drain_shares, 0)


def shards(dosage, weight_tiles, first_tile, last_tile):
    samples, depth = dosage.shape
    gene = weight_tiles.shape[2]
    part = samples // PARTS
    dma = pltpu.SemaphoreType.DMA
    vmem = pl.BlockSpec(memory_space=pltpu.VMEM)
    return pl.pallas_call(
        kernel,
        out_shape=jax.ShapeDtypeStruct((2 * gene, gene), F32),
        in_specs=[pl.BlockSpec(memory_space=pltpu.HBM)] * 4,
        out_specs=vmem,
        scratch_shapes=[
            pltpu.VMEM((samples, depth), BF16),
            pltpu.VMEM((3, depth, gene), BF16),
            pltpu.VMEM((1, gene), jnp.int32),
            pltpu.VMEM((1, gene), jnp.int32),
            pltpu.VMEM((depth, gene), BF16),
            pltpu.VMEM((depth // 2, gene), BF16),
            pltpu.VMEM((depth // 2, gene), BF16),
            pltpu.VMEM((depth, gene), BF16),
            pltpu.VMEM((depth, gene), BF16),
            pltpu.VMEM((samples, gene), F32),
            pltpu.VMEM((samples, gene), F32),
            pltpu.VMEM((samples, gene), F32),
            pltpu.VMEM((samples, gene), F32),
            pltpu.VMEM((samples, gene), F32),
            pltpu.VMEM((2 * samples, 2 * gene), BF16),
            pltpu.VMEM((ZS // 2, 2 * PARTS, gene, part), BF16),
            pltpu.VMEM((ZS // 2, gene, 2 * gene), F32),
            pltpu.VMEM((2, XS, gene, 2 * gene), F32),
            pltpu.VMEM((2, 2, gene, gene), F32),
            pltpu.VMEM((3, gene, gene), F32),
            pltpu.VMEM((PARTS, gene, part), BF16),
            dma((6,)), dma((2,)), dma((2,)), dma((2,)), dma((2,)),
            dma((2,)), dma((2,)), dma((PARTS,)), dma((PARTS,)),
            dma((3, 2)), dma((3, 2)),
            dma((2, 4, 2 * PARTS)), dma((2, 5, 2 * PARTS)),
            dma((3, PARTS)), dma((PARTS,)),
            dma((ZS // 2,)), dma((2, XS)),
            dma((3,)), dma((3,)),
        ],
        compiler_params=pltpu.CompilerParams(
            collective_id=0, has_side_effects=True, vmem_limit_bytes=60 * 2**20
        ),
    )(dosage, weight_tiles, first_tile.reshape(1, gene), last_tile.reshape(1, gene))


def solution(mesh):
    return jax.shard_map(
        shards,
        mesh=mesh,
        in_specs=(P("seg", "loop"), P(None, None, "loop"), P("loop"), P("loop")),
        out_specs=P("seg", "loop"),
        check_vma=False,
    )
```

```python
import functools

import jax
import jax.numpy as jnp
from jax import lax
from jax.experimental import pallas as pl
from jax.experimental.pallas import tpu as pltpu
from jax.sharding import PartitionSpec as P

MESH = pl.DeviceIdType.MESH
F32 = jnp.float32
BF16 = jnp.bfloat16
XS, ZS = 4, 16


def device(x, t, lo, z, c):
    return {"loop": 2 * z + t, "seg": 4 * x + 2 * lo + c}


ORDER = (0, 1, 4, 2, 5, 3, 6, 7)
PARTS = 4


def reach(flow, j):
    return 8 - flow


def kernel(
    dosage_hbm, tiles_hbm, first_hbm, last_hbm, out,
    dosage, tiles, first, last,
    mine, send_a, send_b, tile_a, tile_b,
    part_y, part_z, got_y, got_z, held,
    columns, rows, shares, across, summed, arrived, landed,
    isem, wsend, wrecv, csend, crecv, psend, precv, zsend, zrecv,
    qsend, qrecv, rsend, rrecv, osend, orecv,
    xsend, xrecv, ysend, yrecv,
):
    loop, seg = lax.axis_index("loop"), lax.axis_index("seg")
    z, t = loop // 2, loop % 2
    x, lo, c = seg // 4, (seg // 2) % 2, seg % 2
    sign = 1 - 2 * t
    z_fore, z_back = (z + sign + ZS) % ZS, (z - sign + ZS) % ZS
    fore, back = device(x, t, lo, z_fore, c), device(x, t, lo, z_back, c)
    fore_twin, back_twin = device(x, t, lo, z_fore, 1 - c), device(x, t, lo, z_back, 1 - c)
    twin = device(x, t, lo, z, 1 - c)
    pair = device(x, 1 - t, lo, z, c)
    near = device(x, 1 - t, 1 - lo, z, c)
    near_back = device(x, 1 - t, 1 - lo, z_back, c)
    side = device(x, t, 1 - lo, z, c)
    samples, depth = dosage.shape
    gene = tiles.shape[2]
    part = samples // PARTS
    half = samples // 2

    barrier = pltpu.get_barrier_semaphore()
    partners = [fore, back, fore_twin, back_twin, twin, pair, near, near_back, side]
    partners += [device((x + k) % XS, t, lo, z, c) for k in range(1, XS)]
    for partner in partners:
        pl.semaphore_signal(barrier, inc=1, device_id=partner, device_id_type=MESH)

    piece = pl.ds(pl.multiple_of(c * (depth // 2), depth // 2), depth // 2)
    slot_b, slot_a = 2 * t, 2 - 2 * t
    loads = [
        pltpu.make_async_copy(src, dst, isem.at[i])
        for i, (src, dst) in enumerate((
            (first_hbm, first), (last_hbm, last),
            (tiles_hbm.at[slot_b, piece], tiles.at[slot_b, piece]),
            (tiles_hbm.at[slot_a, piece], tiles.at[slot_a, piece]),
            (tiles_hbm.at[1], tiles.at[1]), (dosage_hbm, dosage),
        ))
    ]
    for load in loads:
        load.start()

    def remote(src, dst, send, recv, to):
        return pltpu.make_async_remote_copy(
            src_ref=src, dst_ref=dst, send_sem=send, recv_sem=recv,
            device_id=to, device_id_type=MESH,
        )

    loads[0].wait()
    loads[1].wait()
    low, high = first[...], last[...]

    def mask(slot):
        block = loop + slot - 1
        ok = (low <= slot) & (high >= slot) & (block >= 0) & (block < 2 * ZS)
        return jnp.where(ok, 1.0, 0.0).astype(BF16)

    loads[2].wait()
    send_b[...] = tiles[slot_b, piece, :] * mask(slot_b)
    pl.semaphore_wait(barrier, len(partners))

    give_b = remote(send_b, tile_b.at[piece], wsend.at[0], wrecv.at[0], near_back)
    give_b.start()
    loads[3].wait()
    send_a[...] = tiles[slot_a, piece, :] * mask(slot_a)
    give_a = remote(send_a, tile_a.at[piece], wsend.at[1], wrecv.at[1], near)
    give_a.start()
    loads[4].wait()
    mine[...] = tiles[1] * mask(1)
    loads[5].wait()
    partials = []

    def send_partials():
        for k in range(2):
            span = pl.ds(k * half, half)
            copy = remote(part_y.at[span], got_y.at[span], psend.at[k], precv.at[k], pair)
            copy.start()
            partials.append(copy)

    part_y[...] = jnp.dot(dosage[...], mine[...], preferred_element_type=F32)
    swap_b = remote(tile_b.at[piece], tile_b.at[piece], csend.at[0], crecv.at[0], twin)
    swap_a = remote(tile_a.at[piece], tile_a.at[piece], csend.at[1], crecv.at[1], twin)
    give_b.wait_recv()
    swap_b.start()
    send_partials()
    swap_b.wait_recv()
    halos = []
    for k in range(PARTS):
        span = pl.ds(k * part, part)
        part_z[span, :] = jnp.dot(dosage[span, :], tile_b[...], preferred_element_type=F32)
        copy = remote(part_z.at[span], got_z.at[span], zsend.at[k], zrecv.at[k], back)
        copy.start()
        halos.append(copy)
    give_a.wait_recv()
    swap_a.start()
    swap_a.wait_recv()
    held[...] = jnp.dot(dosage[...], tile_a[...], preferred_element_type=F32)

    lead = (z + c) % 2 == 0
    cols_own = pl.ds(pl.multiple_of((1 - t) * gene, gene), gene)
    cols_other = pl.ds(pl.multiple_of(t * gene, gene), gene)
    place = z // 2

    def ring(block, flow, step, j, to):
        chunk = rows.at[block, j]
        return remote(
            chunk, chunk, rsend.at[flow, step // 2, j], rrecv.at[flow, (step + 1) // 2, j], to
        )

    def enter(k, flow, to):
        return remote(
            landed.at[k], rows.at[place, PARTS + k], osend.at[flow, k],
            rrecv.at[flow, 0, PARTS + k], to,
        )

    def enter_twin(k):
        return remote(
            landed.at[k], rows.at[place, PARTS + k], osend.at[2, k], orecv.at[k], twin
        )

    locals_ = []
    for k in range(PARTS):
        span = pl.ds(k * part, part)
        if k % 2 == 0:
            partials[k // 2].wait_recv()
        halos[k].wait_recv()
        value = held[span, :] + got_y[span, :] + got_z[span, :]
        turned = value.T.astype(BF16)

        @pl.when(lead)
        def _():
            rows[place, k] = turned
            ring(place, 0, 0, k, fore).start()
            ring(place, 1, 0, k, back).start()

        @pl.when(jnp.logical_not(lead))
        def _():
            landed[k] = turned
            enter(k, 0, fore_twin).start()
            enter(k, 1, back_twin).start()
            enter_twin(k).start()

        columns[span, cols_own] = value.astype(BF16)
        if k % 2 == 1:
            i = k // 2
            here = columns.at[pl.ds(i * half, half), cols_own]
            copy = remote(here, here, qsend.at[0, i], qrecv.at[0, i], pair)
            copy.start()
            locals_.append(copy)
            there = columns.at[pl.ds(samples + i * half, half), cols_own]
            copy = remote(here, there, qsend.at[1, i], qrecv.at[1, i], twin)
            copy.start()
            locals_.append(copy)

    def share(block):
        turned = jnp.concatenate([rows[block, j] for j in range(2 * PARTS)], axis=1)
        value = jnp.dot(turned, columns[...], preferred_element_type=F32)
        for way in range(2):
            shares[block, way] = value[:, way * gene:(way + 1) * gene]
        home = block // 2

        @pl.when(home != x)
        def _():
            for way in range(2):
                remote(
                    shares.at[block, way], across.at[block % 2, x, way], xsend.at[block, way],
                    xrecv.at[block % 2, x, way], device(home, t, lo, z, c),
                ).start()

    odd = (z + c) % 2

    def pass_on(step, far, close):
        for j in ORDER:
            for flow, block, to in ((0, far, fore), (1, close, back)):
                @pl.when((step >= 1) & (step <= reach(flow, j)))
                def _():
                    ring(block, flow, step - 1, j, to).wait_recv()

                @pl.when((step >= 1) & (step < reach(flow, j)))
                def _():
                    ring(block, flow, step, j, to).start()

    def spots(step):
        return (z - sign * step + 2 * ZS) % ZS // 2, (z + sign * step + 2 * ZS) % ZS // 2

    pass_on(odd, *spots(odd))
    relays = []
    for i in range(2):
        got = columns.at[pl.ds(i * half, half), cols_other]
        remote(got, got, qsend.at[0, i], qrecv.at[0, i], pair).wait_recv()
        there = columns.at[pl.ds(samples + i * half, half), cols_other]
        copy = remote(got, there, qsend.at[2, i], qrecv.at[2, i], twin)
        copy.start()
        relays.append(copy)
    for copy in (locals_[1], locals_[3], *relays):
        copy.wait_recv()

    @pl.when(lead)
    def _():
        for k in range(PARTS):
            enter_twin(k).wait_recv()
        share(place)

    @pl.when(jnp.logical_not(lead))
    def _():
        for block in spots(1):
            share(block)

    def travel(i, carry):
        step = 2 * i + odd
        far, close = spots(step)
        pass_on(step, far, close)

        @pl.when(step <= 8)
        def _():
            share(far)

        @pl.when(step <= 7)
        def _():
            share(close)

        return carry

    lax.fori_loop(1, 5, travel, 0)

    def away(block):
        gap = (2 * block + c - z + ZS) % ZS
        return jnp.minimum(gap, ZS - gap)

    swapped = (away(2 * x) > away(2 * x + 1)).astype(jnp.int32)

    def ysend_copy(index, block_lo, to_t, to_lo):
        return remote(
            summed.at[block_lo, to_t], arrived.at[index], ysend.at[index], yrecv.at[index],
            device(x, to_t, to_lo, z, c),
        )

    same = ysend_copy(0, lo, 1 - t, lo)
    cross = ysend_copy(1, 1 - lo, t, 1 - lo)
    both = ysend_copy(2, 1 - lo, 1 - t, 1 - lo)
    for turn in range(2):
        other = (swapped + turn) % 2
        block = 2 * x + other
        for way in range(2):
            for k in range(1, XS):
                source = (x + k) % XS
                remote(
                    shares.at[block, way], across.at[other, source, way], xsend.at[block, way],
                    xrecv.at[other, source, way], twin,
                ).wait_recv()
            total = shares[block, way]
            for k in range(1, XS):
                total = total + across[other, (x + k) % XS, way]
            summed[other, way] = total

            @pl.when((other == lo) & (way != t))
            def _():
                same.start()

            @pl.when((other != lo) & (way != t))
            def _():
                both.start()

            @pl.when((other != lo) & (way == t))
            def _():
                cross.start()

    scale = 1.0 / (samples * XS * 4)
    own_rows = pl.ds(pl.multiple_of((1 - t) * gene, gene), gene)
    other_rows = pl.ds(pl.multiple_of(t * gene, gene), gene)
    cross.wait_recv()
    out[own_rows, :] = (summed[lo, t] + arrived[1]) * scale
    same.wait_recv()
    both.wait_recv()
    out[other_rows, :] = (arrived[0] + arrived[2]) * scale

    for copy in (
        give_a, give_b, swap_a, swap_b, *partials, *halos, *locals_, *relays, same, cross, both
    ):
        copy.wait_send()

    @pl.when(jnp.logical_not(lead))
    def _():
        for k in range(PARTS):
            enter(k, 0, fore_twin).wait_send()
            enter(k, 1, back_twin).wait_send()
            enter_twin(k).wait_send()

    @pl.when(lead)
    def _():
        for k in range(PARTS):
            ring(place, 0, 0, k, fore).wait_send()
            ring(place, 1, 0, k, back).wait_send()

    def drain(i, carry):
        step = 2 * i + odd
        for j in range(2 * PARTS):
            for flow, to in ((0, fore), (1, back)):
                @pl.when((step >= 1) & (step < reach(flow, j)))
                def _():
                    ring(place, flow, step, j, to).wait_send()

        return carry

    lax.fori_loop(0, 4, drain, 0)

    def drain_shares(block, carry):
        @pl.when(block // 2 != x)
        def _():
            for way in range(2):
                remote(
                    shares.at[block, way], across.at[0, 0, way], xsend.at[block, way],
                    xrecv.at[0, 0, way], twin,
                ).wait_send()

        return carry

    lax.fori_loop(0, ZS // 2, drain_shares, 0)


def shards(dosage, weight_tiles, first_tile, last_tile):
    samples, depth = dosage.shape
    gene = weight_tiles.shape[2]
    part = samples // PARTS
    dma = pltpu.SemaphoreType.DMA
    vmem = pl.BlockSpec(memory_space=pltpu.VMEM)
    return pl.pallas_call(
        kernel,
        out_shape=jax.ShapeDtypeStruct((2 * gene, gene), F32),
        in_specs=[pl.BlockSpec(memory_space=pltpu.HBM)] * 4,
        out_specs=vmem,
        scratch_shapes=[
            pltpu.VMEM((samples, depth), BF16),
            pltpu.VMEM((3, depth, gene), BF16),
            pltpu.VMEM((1, gene), jnp.int32),
            pltpu.VMEM((1, gene), jnp.int32),
            pltpu.VMEM((depth, gene), BF16),
            pltpu.VMEM((depth // 2, gene), BF16),
            pltpu.VMEM((depth // 2, gene), BF16),
            pltpu.VMEM((depth, gene), BF16),
            pltpu.VMEM((depth, gene), BF16),
            pltpu.VMEM((samples, gene), F32),
            pltpu.VMEM((samples, gene), F32),
            pltpu.VMEM((samples, gene), F32),
            pltpu.VMEM((samples, gene), F32),
            pltpu.VMEM((samples, gene), F32),
            pltpu.VMEM((2 * samples, 2 * gene), BF16),
            pltpu.VMEM((ZS // 2, 2 * PARTS, gene, part), BF16),
            pltpu.VMEM((ZS // 2, 2, gene, gene), F32),
            pltpu.VMEM((2, XS, 2, gene, gene), F32),
            pltpu.VMEM((2, 2, gene, gene), F32),
            pltpu.VMEM((3, gene, gene), F32),
            pltpu.VMEM((PARTS, gene, part), BF16),
            dma((6,)), dma((2,)), dma((2,)), dma((2,)), dma((2,)),
            dma((2,)), dma((2,)), dma((PARTS,)), dma((PARTS,)),
            dma((3, 2)), dma((3, 2)),
            dma((2, 4, 2 * PARTS)), dma((2, 5, 2 * PARTS)),
            dma((3, PARTS)), dma((PARTS,)),
            dma((ZS // 2, 2)), dma((2, XS, 2)),
            dma((3,)), dma((3,)),
        ],
        compiler_params=pltpu.CompilerParams(
            collective_id=0, has_side_effects=True, vmem_limit_bytes=54800 * 1024
        ),
    )(dosage, weight_tiles, first_tile.reshape(1, gene), last_tile.reshape(1, gene))


def solution(mesh):
    return jax.shard_map(
        shards,
        mesh=mesh,
        in_specs=(P("seg", "loop"), P(None, None, "loop"), P("loop"), P("loop")),
        out_specs=P("seg", "loop"),
        check_vma=False,
    )
```
